512 devices in a mesh: dp: 32 (over x, z_lo, core), seq: 16 (over z_hi, y).
Axes of the slice: x: 4, y: 8, z: 8 (z_hi: 2, z_lo: 4; z = z_hi * 4 + z_lo), core: 2. Of those that a mesh axis runs over, the one named last changes fastest.
Arguments:
- q_space: bfloat16 [32, 2560, 1152], P('dp', 'seq'), may hold values from -64 to 64
- k_space: bfloat16 [32, 2560, 1152], P('dp', 'seq'), may hold values from -6 to 6
- v_space: bfloat16 [32, 2560, 1152], P('dp', 'seq'), may hold values from -6 to 6
- q_time: bfloat16 [32, 2560, 1152], P('dp', 'seq'), may hold values from -64 to 64
- k_time: bfloat16 [32, 2560, 1152], P('dp', 'seq'), may hold values from -6 to 6
- v_time: bfloat16 [32, 2560, 1152], P('dp', 'seq'), may hold values from -6 to 6
- weight: bfloat16 [1152, 1152], P('dp'), may hold values from -0.1875 to 0.1875
- target: bfloat16 [32, 2560, 1152], P('dp', 'seq'), may hold values from -6 to 6
Outputs:
- grad_q_space: bfloat16 [32, 2560, 1152], P('dp', 'seq')
- grad_k_space: bfloat16 [32, 2560, 1152], P('dp', 'seq')
- grad_v_space: bfloat16 [32, 2560, 1152], P('dp', 'seq')
- grad_q_time: bfloat16 [32, 2560, 1152], P('dp', 'seq')
- grad_k_time: bfloat16 [32, 2560, 1152], P('dp', 'seq')
- grad_v_time: bfloat16 [32, 2560, 1152], P('dp', 'seq')
- weight_grad: float32 [1152, 1152], P('seq')
The draws below stay inside these ranges and needn't reach their ends.
All inputs are finite; a program needn't handle non-finite values.
Results may differ from the reference program's by a relative error of at most 0.025.
Values may be sent and summed in bfloat16 or wider, within the bound.
A program may use at most 64 MiB of HBM per device.

```python
import math
import jax
import jax.numpy as jnp
from jax import lax

D = 1152
HEADS = 16
HEAD_DIM = 72
PATCHES = 160
FRAMES = 16
TOKENS = 2560
CLIPS = 32
N_SEQ = 16


def pair_space(base_key):
    folded = jax.random.fold_in(base_key, 101)
    query_key, key_key = jax.random.split(folded, 2)
    layout = (CLIPS, FRAMES, PATCHES, D)
    queries = jnp.clip(jax.random.normal(query_key, layout, jnp.float32), -6.0, 6.0)
    key_data = jnp.clip(jax.random.normal(key_key, layout, jnp.float32), -6.0, 6.0)
    return (queries.reshape(CLIPS, FRAMES * PATCHES, D), key_data.reshape(CLIPS, FRAMES * PATCHES, D))


def pair_time(base_key):
    folded = jax.random.fold_in(base_key, 202)
    query_key, key_key = jax.random.split(folded, 2)
    layout = (CLIPS, FRAMES, PATCHES, D)
    queries = jnp.clip(jax.random.normal(query_key, layout, jnp.float32), -6.0, 6.0)
    key_data = jnp.clip(jax.random.normal(key_key, layout, jnp.float32), -6.0, 6.0)
    return (queries.reshape(CLIPS, FRAMES * PATCHES, D), key_data.reshape(CLIPS, FRAMES * PATCHES, D))


def draw_q_space(key, part):
    return pair_space(key)[0].astype(jnp.bfloat16)


def draw_k_space(key, part):
    return pair_space(key)[1].astype(jnp.bfloat16)


def draw_q_time(key, part):
    return pair_time(key)[0].astype(jnp.bfloat16)


def draw_k_time(key, part):
    return pair_time(key)[1].astype(jnp.bfloat16)


def levels(key, extent, cuts, smallest, largest):
    def one(axis_at, shards_of):
        heights = jax.random.uniform(jax.random.fold_in(jax.random.fold_in(key, 6), axis_at), (shards_of,), jnp.float32, smallest / len(cuts), largest / len(cuts))
        return jnp.repeat(jnp.exp(heights), extent[axis_at] // shards_of).reshape((-1,) + (1,) * (len(extent) - axis_at - 1))

    loudness = one(*cuts[0])
    for cut in cuts[1:]:
        loudness = loudness * one(*cut)
    return loudness


def centred(rng, dims, scale, limit, cuts=(), held_as=jnp.bfloat16):
    drawn = jax.random.normal(rng, dims, jnp.float32) * scale
    if len(cuts) > 0:
        drawn = levels(rng, dims, cuts, -0.22, 0.18) * drawn
    return jnp.clip(drawn, min=-limit, max=limit).astype(held_as)


def setup_inputs(seed: int = 0) -> dict:
    splits = jax.random.split(jax.random.key(seed), 9)
    q_space = draw_q_space(jax.random.fold_in(splits[8], 71), 0)
    k_space = draw_k_space(jax.random.fold_in(splits[8], 71), 0)
    v_space = centred(splits[2], (CLIPS, TOKENS, D), 1.0, 6.0, ((0, 32), (1, 16)))
    q_time = draw_q_time(jax.random.fold_in(splits[8], 71), 0)
    k_time = draw_k_time(jax.random.fold_in(splits[8], 71), 0)
    v_time = centred(splits[5], (CLIPS, TOKENS, D), 1.0, 6.0, ((0, 32), (1, 16)))
    weight = centred(splits[6], (D, D), D ** -0.5, 0.1875, ((0, 32),))
    target = centred(splits[7], (CLIPS, TOKENS, D), 1.0, 6.0, ((0, 32), (1, 16)))
    return {"q_space": q_space, "k_space": k_space, "v_space": v_space, "q_time": q_time, "k_time": k_time, "v_time": v_time, "weight": weight, "target": target}


def form_pair(layout):
    if layout == 'space':
        return ('blhe', 'bmhe')
    return ('lbhe', 'mbhe')

def product(pattern, left, right):
    return jnp.einsum(pattern, left.astype(jnp.float32), right.astype(jnp.float32), precision=lax.Precision.HIGHEST)

def attend_forward(query, key_data, values, layout):
    query_form, key_form = form_pair(layout)
    scaling = 1.0 / math.sqrt(HEAD_DIM)
    logits = product(query_form + ',' + key_form + '->bhlm', query, key_data) * scaling
    row_max = lax.optimization_barrier(jnp.max(logits, axis=-1, keepdims=True))
    lifted = jnp.exp(logits - row_max)
    attention = lifted / lax.optimization_barrier(jnp.sum(lifted, axis=-1, keepdims=True))
    rounded = attention.astype(jnp.bfloat16)
    result = product('bhlm,' + key_form + '->' + query_form, rounded, values)
    return (attention, rounded, result)

def attend_backward(query, key_data, values, attention, rounded, step_grad, layout):
    query_form, key_form = form_pair(layout)
    scaling = 1.0 / math.sqrt(HEAD_DIM)
    upstream = product(query_form + ',' + key_form + '->bhlm', step_grad, values)
    grad_values = product('bhlm,' + query_form + '->' + key_form, rounded, step_grad).astype(jnp.bfloat16)
    grad_scores = (attention * (upstream - lax.optimization_barrier(jnp.sum(attention * upstream, axis=-1, keepdims=True)))).astype(jnp.bfloat16)
    grad_query = (product('bhlm,' + key_form + '->' + query_form, grad_scores, key_data) * scaling).astype(jnp.bfloat16)
    grad_keys = (product('bhlm,' + query_form + '->' + key_form, grad_scores, query) * scaling).astype(jnp.bfloat16)
    return (grad_query, grad_keys, grad_values)

def split_heads(array):
    return array.reshape(FRAMES, PATCHES, HEADS, HEAD_DIM)

def one_clip(weight, arrays):
    space_q, space_k, space_v, time_q, time_k, time_v, target_rows = [split_heads(item) for item in arrays]
    attention_s, rounded_s, result_s = attend_forward(space_q, space_k, space_v, 'space')
    attention_t, rounded_t, result_t = attend_forward(time_q, time_k, time_v, 'time')
    out_space = result_s.astype(jnp.bfloat16)
    combined = (out_space.astype(jnp.float32) + result_t).astype(jnp.bfloat16).reshape(TOKENS, D)
    projected = jnp.dot(combined, weight, preferred_element_type=jnp.float32)
    output_grad = (projected - target_rows.reshape(TOKENS, D).astype(jnp.float32)).astype(jnp.bfloat16)
    step_grad = jnp.dot(output_grad, weight.T, preferred_element_type=jnp.float32).astype(jnp.bfloat16)
    step_heads = split_heads(step_grad)
    grads_space = attend_backward(space_q, space_k, space_v, attention_s, rounded_s, step_heads, 'space')
    grads_time = attend_backward(time_q, time_k, time_v, attention_t, rounded_t, step_heads, 'time')
    blocks = combined.reshape(FRAMES, N_SEQ, PATCHES // N_SEQ, D)
    grad_blocks = output_grad.reshape(FRAMES, N_SEQ, PATCHES // N_SEQ, D)
    partials = product('fnpi,fnpc->nic', blocks, grad_blocks)
    partials_b = lax.optimization_barrier(partials.astype(jnp.bfloat16))
    partial_sum = lax.optimization_barrier(jnp.sum(partials_b.astype(jnp.float32), axis=0))
    outputs = [item.reshape(TOKENS, D) for item in grads_space + grads_time]
    return tuple(outputs) + (partial_sum,)

def reference(q_space, k_space, v_space, q_time, k_time, v_time, weight, target):
    results = lax.map(lambda arrays: one_clip(weight, arrays), (q_space, k_space, v_space, q_time, k_time, v_time, target))
    weight_grad = lax.optimization_barrier(jnp.sum(results[6], axis=0)) * (1.0 / math.sqrt(CLIPS * TOKENS))
    return (results[0], results[1], results[2], results[3], results[4], results[5], weight_grad)
```

```python
import functools
import math

import jax
import jax.numpy as jnp
from jax import lax
from jax.experimental import pallas as pl
from jax.experimental.pallas import tpu as pltpu
from jax.sharding import PartitionSpec as P

HEADS = 16
HEAD_DIM = 72
D = 1152
TOK = 160
MAIN = 128
SCALING = 1.0 / math.sqrt(HEAD_DIM)
BF = jnp.bfloat16
F32 = jnp.float32
MESH = pl.DeviceIdType.MESH
MQ, MK, MV, MTQ, MA, MTA, MO, MTO, MG, MTG = 0, 1, 2, 3, 4, 5, 6, 7, 8, 17
N_MSG = 18


def dot_nn(a, b):
    return lax.dot_general(a, b, (((1,), (0,)), ((), ())), preferred_element_type=F32)


def dot_nt(a, b):
    return lax.dot_general(a, b, (((1,), (1,)), ((), ())), preferred_element_type=F32)


def dot_tn(a, b):
    return lax.dot_general(a, b, (((0,), (0,)), ((), ())), preferred_element_type=F32)


def window(head):
    start = jnp.minimum((9 * head) // 16, 7) * 128
    lanes = lax.broadcasted_iota(jnp.int32, (1, 256), 1) + start
    inside = jnp.logical_and(lanes >= HEAD_DIM * head, lanes < HEAD_DIM * head + HEAD_DIM)
    return pl.ds(pl.multiple_of(start, 128), 256), inside


def get(ref, cols):
    value = ref[:, :, cols]
    return value.reshape(8 * ref.shape[0], value.shape[2])


def put(ref, cols, value):
    ref[:, :, cols] = value.astype(BF).reshape(ref.shape[0], 8, value.shape[1])


def put_head(ref, cols, inside, value):
    put(ref, cols, jnp.where(inside, value, get(ref, cols).astype(F32)))


def forward_head(head, q_ref, k_ref, v_ref, bias_ref, probs_ref, out_ref):
    cols, inside = window(head)
    chosen = inside.astype(F32).astype(BF)
    logits = dot_nt(get(q_ref, cols) * chosen, get(k_ref, cols)) * SCALING
    if bias_ref is not None:
        logits = logits + bias_ref[...]
    lifted = jnp.exp(logits - jnp.max(logits, axis=-1, keepdims=True))
    probs = lifted * (1.0 / jnp.sum(lifted, axis=-1, keepdims=True))
    probs_ref[head] = probs
    put_head(out_ref, cols, inside, dot_nn(probs.astype(BF), get(v_ref, cols)))


def backward_head(head, q_ref, k_ref, v_ref, probs_ref, step_ref, gq_ref, gk_ref, gv_ref):
    cols, inside = window(head)
    chosen = inside.astype(F32).astype(BF)
    step = get(step_ref, cols)
    probs = probs_ref[head]
    upstream = dot_nt(step * chosen, get(v_ref, cols))
    put_head(gv_ref, cols, inside, dot_tn(probs.astype(BF), step))
    scores = (probs * (upstream - jnp.sum(probs * upstream, axis=-1, keepdims=True))).astype(BF)
    put_head(gq_ref, cols, inside, dot_nn(scores, get(k_ref, cols)) * SCALING)
    put_head(gk_ref, cols, inside, dot_tn(scores, get(q_ref, cols)) * SCALING)


def for_heads(first, last, step):
    def pair(i, carry):
        step(first + 2 * i)
        step(first + 2 * i + 1)
        return carry

    lax.fori_loop(0, (last - first) // 2, pair, 0)


def iota(shape, axis):
    return lax.broadcasted_iota(jnp.int32, shape, axis)


def kernel(
    qs, ks, vs, qt, kt, vt, w_own, target,
    gqs, gks, gvs, gqt, gkt, gvt, wg,
    wb, w, rq, rk, rv, ra, rtq, rta, tq, ta, to, tg, space, over, step_b, step_f,
    ot, ro, rto, comb, gradp, gq, gk, gv, rgq, rgk, rgv, rtg, probs_s, probs_t, bias,
    wgp, r1, half, r2, h2, r3, h3, r4, h4, r5,
    ssem, rsem, wsend, wrecv, csend, crecv, rsend, rrecv,
):
    dp = lax.axis_index("dp")
    s = lax.axis_index("seq")
    core = lax.rem(dp, 2)
    chip = dp // 2
    x = chip // 4
    zl = lax.rem(chip, 4)
    zh = s // 8
    y = lax.rem(s, 8)

    def device(x_, zl_, core_, zh_, y_):
        return ((x_ * 4 + zl_) * 2 + core_, zh_ * 8 + y_)

    def plus(value, k, n):
        return lax.rem(value + k, n)

    sibling = device(x, zl, 1 - core, zh, y)

    barrier = pltpu.get_barrier_semaphore()

    def greet(who):
        pl.semaphore_signal(barrier, inc=1, device_id=who, device_id_type=MESH)

    for k in range(1, 16):
        greet((dp, plus(s, k, 16)))
    for k in range(1, 4):
        greet(device(x, plus(zl, k, 4), core, zh, y))
        greet(device(x, plus(zl, k, 4), core, 1 - zh, y))
        greet(device(plus(x, k, 4), zl, core, zh, y))
        greet(device(plus(x, k, 4), zl, 1 - core, zh, y))
    greet(sibling)
    pl.semaphore_wait(barrier, 28)

    def to_peer(msg, src, dst, peer, cols=None):
        a, b = src.at[peer], dst.at[s]
        if cols is not None:
            a, b = src.at[peer, :, cols], dst.at[s, :, cols]
        return pltpu.make_async_remote_copy(
            src_ref=a, dst_ref=b, send_sem=ssem.at[msg, peer], recv_sem=rsem.at[msg, s],
            device_id=(dp, peer), device_id_type=MESH,
        )

    def from_peer(msg, src, dst, peer, cols=None):
        a, b = src.at[peer], dst.at[peer]
        if cols is not None:
            a, b = src.at[peer, :, cols], dst.at[peer, :, cols]
        return pltpu.make_async_remote_copy(
            src_ref=a, dst_ref=b, send_sem=ssem.at[msg, peer], recv_sem=rsem.at[msg, peer],
            device_id=(dp, peer), device_id_type=MESH,
        )

    def scatter(items):
        def one(k, carry):
            peer = plus(s, k, 16)
            for msg, src, dst, cols in items:
                to_peer(msg, src, dst, peer, cols).start()
            return carry

        lax.fori_loop(1, 16, one, 0)
        for msg, src, dst, cols in items:
            if cols is None:
                dst[s] = src[s]
            else:
                dst[s, :, cols] = src[s, :, cols]

    def gathered(items):
        def one(k, carry):
            peer = plus(s, k, 16)
            for msg, src, dst, cols in items:
                from_peer(msg, src, dst, peer, cols).wait_recv()
            return carry

        lax.fori_loop(1, 16, one, 0)

    def drained(items):
        def one(k, carry):
            peer = plus(s, k, 16)
            for msg, src, dst, cols in items:
                to_peer(msg, src, dst, peer, cols).wait_send()
            return carry

        lax.fori_loop(1, 16, one, 0)

    qkv_items = [(MQ, qt, rq, None), (MK, kt, rk, None), (MV, vt, rv, None)]
    tq_items = [(MTQ, tq, rtq, None)]
    a_items = [(MA, over, ra, None), (MTA, ta, rta, None)]
    o_items = [(MO, ot, ro, None), (MTO, to, rto, None)]
    thirds = [pl.ds(384 * c, 384) for c in range(3)]
    g_items = [
        [
            (MG + 3 * c, gq, rgq, thirds[c]),
            (MG + 3 * c + 1, gk, rgk, thirds[c]),
            (MG + 3 * c + 2, gv, rgv, thirds[c]),
        ]
        for c in range(3)
    ]
    tg_items = [(MTG, tg, rtg, None)]

    def w_copy(src, slot, k, who):
        return pltpu.make_async_remote_copy(
            src_ref=src, dst_ref=wb.at[core, slot], send_sem=wsend.at[k], recv_sem=wrecv.at[slot],
            device_id=who, device_id_type=MESH,
        )

    def w_start():
        for k in range(1, 4):
            w_copy(w_own, chip, k - 1, device(x, plus(zl, k, 4), core, zh, y)).start()
        for k in range(1, 4):
            w_copy(w_own, chip, 2 + k, device(plus(x, k, 4), zl, core, zh, y)).start()
        wb[core, chip] = w_own[...]

    def w_core(group):
        part = wb.at[core, pl.ds(4 * group, 4)]
        return pltpu.make_async_remote_copy(
            src_ref=part, dst_ref=part, send_sem=csend.at[group], recv_sem=crecv.at[group],
            device_id=sibling, device_id_type=MESH,
        )

    def w_other(group):
        part = wb.at[1 - core, pl.ds(4 * group, 4)]
        return pltpu.make_async_remote_copy(
            src_ref=part, dst_ref=part, send_sem=csend.at[group], recv_sem=crecv.at[group],
            device_id=sibling, device_id_type=MESH,
        )

    def w_forward():
        for j in range(1, 4):
            slot = x * 4 + plus(zl, j, 4)
            part = wb.at[core, slot]
            w_copy(part, slot, 0, sibling).wait_recv()
            for k in range(1, 4):
                who = device(plus(x, k, 4), zl, core, zh, y)
                w_copy(part, slot, 3 * j + 2 + k, who).start()
        w_core(x).start()

    def w_share():
        for k in range(1, 4):
            group = plus(x, k, 4)
            for j in range(4):
                slot = group * 4 + j
                w_copy(wb.at[core, slot], slot, 0, sibling).wait_recv()
            w_core(group).start()

    def w_finish():
        for group in range(4):
            w_other(group).wait_recv()

        def lay(i, carry):
            slots = [wb[0, 2 * i], wb[1, 2 * i], wb[0, 2 * i + 1], wb[1, 2 * i + 1]]
            w[pl.ds(pl.multiple_of(144 * i, 16), 144), :] = jnp.concatenate(slots, axis=0)
            return carry

        lax.fori_loop(0, 8, lay, 0)

    def w_drained():
        for k in range(6):
            w_copy(w_own, chip, k, sibling).wait_send()
        for k in range(6, 15):
            w_copy(w_own, chip, k, sibling).wait_send()
        for group in range(4):
            w_core(group).wait_send()

    def packer():
        i, m = iota((128, 96), 0), iota((128, 96), 1)
        r = lax.rem(i, 8)
        source = 32 * (r // 2) + 2 * (i // 8) + lax.rem(r, 2)
        return jnp.where(jnp.logical_and(m == source, r < 6), 1.0, 0.0).astype(BF)

    def unpacker(k):
        i, m = iota((32, 128), 0), iota((32, 128), 1)
        return jnp.where(m == 8 * (i // 2) + 2 * k + lax.rem(i, 2), 1.0, 0.0).astype(BF)

    every = pl.ds(0, D)

    def last_rows(part, cols):
        value = part[16:20, :, cols]
        return value.reshape(32, value.shape[2])

    def whole(ref):
        return ref[...].reshape(128, ref.shape[2])

    def pack(stack, dst):
        dst[...] = dot_nn(packer(), stack).astype(BF).reshape(dst.shape)

    def unpack(src, k, part, cols):
        part[16:20, :, cols] = dot_nn(unpacker(k), whole(src)).astype(BF).reshape(4, 8, src.shape[2])

    def pack_arrays(parts, dst):
        pack(jnp.concatenate([last_rows(p, every) for p in parts], axis=0), dst)

    def unpack_arrays(src, parts):
        for k, part in enumerate(parts):
            unpack(src, k, part, every)

    def pack_thirds(part, dst):
        pack(jnp.concatenate([last_rows(part, thirds[g]) for g in range(3)], axis=0), dst)

    def unpack_thirds(src, part):
        for g in range(3):
            unpack(src, g, part, thirds[g])

    def in_thirds(step):
        def one(c, carry):
            step(pl.ds(pl.multiple_of(384 * c, 128), 384))
            return carry

        lax.fori_loop(0, 3, one, 0)

    w_start()
    scatter(qkv_items)
    pack_arrays([qt, kt, vt], tq)
    scatter(tq_items)

    i, m = iota((TOK, TOK), 0), iota((TOK, TOK), 1)
    patch_i = jnp.where(i < MAIN, lax.rem(i, 8), 8 + lax.rem(i, 2))
    patch_m = jnp.where(m < MAIN, lax.rem(m, 8), 8 + lax.rem(m, 2))
    bias[...] = jnp.where(patch_i == patch_m, 0.0, -1e30)

    def space_forward(h):
        forward_head(h, qs, ks, vs, None, probs_s, space)

    for_heads(0, 6, space_forward)
    w_forward()
    for_heads(6, 16, space_forward)
    w_share()
    w_finish()

    def project_space(cols):
        product = dot_nn(get(space, every), w[:, cols])
        put(gradp, cols, product - get(target, cols).astype(F32))

    in_thirds(project_space)

    def back_space(cols):
        put(over, cols, dot_nt(get(gradp, every), w[cols, :]))

    in_thirds(back_space)
    pack_thirds(over, ta)
    scatter(a_items)

    gathered(qkv_items)
    gathered(tq_items)
    unpack_arrays(rtq, [rq, rk, rv])
    for_heads(0, 16, lambda h: forward_head(h, rq, rk, rv, bias, probs_t, ot))
    pack_thirds(ot, to)
    scatter(o_items)

    def project_time(cols):
        put(gradp, cols, dot_nn(get(ot, every), w[:, cols]))

    in_thirds(project_time)
    gathered(a_items)
    unpack_thirds(rta, ra)

    def back_time(cols):
        share = dot_nt(get(gradp, every), w[cols, :])
        put(step_b, cols, share + get(ra, cols).astype(F32))

    in_thirds(back_time)

    def time_backward(h):
        backward_head(h, rq, rk, rv, probs_t, step_b, gq, gk, gv)

    def send_grads(c):
        scatter(g_items[c])

    for_heads(0, 6, time_backward)
    send_grads(0)

    gathered(o_items)
    unpack_thirds(rto, ro)
    comb[...] = (space[...].astype(F32) + ro[...].astype(F32)).astype(BF)

    def project_all(cols):
        product = dot_nn(get(comb, every), w[:, cols])
        put(gradp, cols, product - get(target, cols).astype(F32))

    in_thirds(project_all)

    def to_sibling(j):
        rows = pl.ds(pl.multiple_of(576 * (1 - core) + 144 * j, 16), 144)
        return pltpu.make_async_remote_copy(
            src_ref=wgp.at[rows], dst_ref=r1.at[pl.ds(144 * j, 144)],
            send_sem=rsend.at[j], recv_sem=rrecv.at[j], device_id=sibling, device_id_type=MESH,
        )

    def x_window(x_):
        return pl.ds(pl.multiple_of(256 * x_, 128), 384)

    def to_x(j, k):
        x_ = plus(x, k, 4)
        rows = pl.ds(144 * j, 144)
        return pltpu.make_async_remote_copy(
            src_ref=half.at[rows, x_window(x_)], dst_ref=r2.at[k - 1, rows],
            send_sem=rsend.at[4 + 3 * j + k - 1], recv_sem=rrecv.at[4 + 3 * j + k - 1],
            device_id=device(x_, zl, core, zh, y), device_id_type=MESH,
        )

    def to_y(k):
        y_ = plus(y, k, 8)
        return pltpu.make_async_remote_copy(
            src_ref=h2.at[y_], dst_ref=r3.at[k - 1],
            send_sem=rsend.at[15 + k], recv_sem=rrecv.at[15 + k],
            device_id=device(x, zl, core, zh, y_), device_id_type=MESH,
        )

    def to_z(k, same):
        zh_ = zh if same else 1 - zh
        slot = k - 1 if same else 3 + k
        return pltpu.make_async_remote_copy(
            src_ref=h3, dst_ref=r4.at[slot], send_sem=rsend.at[23 + slot],
            recv_sem=rrecv.at[23 + slot], device_id=device(x, plus(zl, k, 4), core, zh_, y),
            device_id_type=MESH,
        )

    def to_all(k, flip):
        slot = k - 1 if flip == 0 else 3 + k
        return pltpu.make_async_remote_copy(
            src_ref=h4, dst_ref=r5.at[x], send_sem=rsend.at[31 + slot], recv_sem=rrecv.at[31 + x],
            device_id=device(plus(x, k, 4), zl, core if flip == 0 else 1 - core, zh, y),
            device_id_type=MESH,
        )

    def from_all(x_):
        return pltpu.make_async_remote_copy(
            src_ref=h4, dst_ref=r5.at[x_], send_sem=rsend.at[31], recv_sem=rrecv.at[31 + x_],
            device_id=sibling, device_id_type=MESH,
        )

    def terms(j, carry):
        rows = pl.ds(pl.multiple_of(128 * j, 128), 128)
        wgp[rows, :] = dot_tn(get(comb, rows), get(gradp, every)).astype(BF)
        return carry

    lax.fori_loop(0, 9, terms, 0)
    for j in range(4):
        to_sibling(j).start()

    def back_all(cols):
        put(step_f, cols, dot_nt(get(gradp, every), w[cols, :]))

    in_thirds(back_all)

    for j in range(4):
        to_sibling(j).wait_recv()
        rows = pl.ds(144 * j, 144)
        own = wgp[pl.ds(pl.multiple_of(576 * core + 144 * j, 16), 144), :]
        half[rows, :] = (own.astype(F32) + r1[rows, :].astype(F32)).astype(BF)
        for k in range(1, 4):
            to_x(j, k).start()

    for_heads(6, 12, time_backward)
    send_grads(1)
    for_heads(12, 16, time_backward)
    send_grads(2)
    pack_arrays([gq, gk, gv], tg)
    scatter(tg_items)

    for j in range(4):
        for k in range(1, 4):
            to_x(j, k).wait_recv()
        for i in range(2):
            rows = pl.ds(144 * j + 72 * i, 72)
            total = half[rows, x_window(x)].astype(F32)
            for k in range(1, 4):
                total = total + r2[k - 1, rows, :].astype(F32)
            h2[2 * j + i] = total.astype(BF)
    for k in range(1, 8):
        to_y(k).start()

    def space_backward(h):
        backward_head(h, qs, ks, vs, probs_s, step_f, gqs, gks, gvs)

    for_heads(0, 8, space_backward)

    total = h2[y].astype(F32)
    for k in range(1, 8):
        to_y(k).wait_recv()
        total = total + r3[k - 1].astype(F32)
    h3[...] = total.astype(BF)

    @pl.when(zh == core)
    def _():
        for k in range(1, 4):
            to_z(k, True).start()

    @pl.when(zh != core)
    def _():
        for k in range(4):
            to_z(k, False).start()

    for_heads(8, 16, space_backward)

    @pl.when(zh == core)
    def _():
        total = h3[...].astype(F32)
        for k in range(1, 4):
            to_z(k, True).wait_recv()
            total = total + r4[k - 1].astype(F32)
        for k in range(4):
            to_z(k, False).wait_recv()
            total = total + r4[3 + k].astype(F32)
        h4[...] = total.astype(BF)
        for k in range(1, 4):
            to_all(k, 0).start()
        for k in range(4):
            to_all(k, 1).start()
        r5[x] = h4[...]
        for k in range(1, 4):
            from_all(plus(x, k, 4)).wait_recv()
        for k in range(1, 4):
            to_z(k, True).wait_send()
            to_all(k, 0).wait_send()
        for k in range(4):
            to_all(k, 1).wait_send()

    @pl.when(zh != core)
    def _():
        for k in range(4):
            from_all(plus(x, k, 4)).wait_recv()
        for k in range(4):
            to_z(k, False).wait_send()

    scale = 1.0 / math.sqrt(81920)
    for c in range(4):
        wide = 256 if c < 3 else 384
        wg[:, pl.ds(256 * c, wide)] = r5[c, :, pl.ds(0, wide)].astype(F32) * scale

    for c in range(3):
        gathered(g_items[c])
    gathered(tg_items)
    for src, dst in ((rgq, gqt), (rgk, gkt), (rgv, gvt)):
        dst[0:16] = src[...]
    unpack_arrays(rtg, [gqt, gkt, gvt])

    drained(qkv_items + tq_items + a_items + o_items + tg_items)
    for c in range(3):
        drained(g_items[c])
    w_drained()
    for j in range(4):
        to_sibling(j).wait_send()
        for k in range(1, 4):
            to_x(j, k).wait_send()
    for k in range(1, 8):
        to_y(k).wait_send()


def shards(q_space, k_space, v_space, q_time, k_time, v_time, weight, target):
    tokens = (q_space, k_space, v_space, q_time, k_time, v_time, target)
    flat = [item.reshape(20, 8, D) for item in tokens]
    vm = pl.BlockSpec(memory_space=pltpu.VMEM)

    def buf(*shape, dtype=BF):
        return pltpu.VMEM(shape, dtype)

    tok = buf(20, 8, D)
    main = buf(16, 8, D)
    third = buf(16, 8, 384)
    scratch = [
        buf(2, 16, 36, D), buf(D, D),
        tok, tok, tok, tok,
        main, third, main, third, third, main,
        tok, tok, tok, tok,
        tok, tok, third, tok, tok,
        tok, tok, tok, main, main, main, main,
        buf(HEADS, TOK, TOK, dtype=F32), buf(HEADS, TOK, TOK, dtype=F32), buf(TOK, TOK, dtype=F32),
        buf(D, D), buf(576, D), buf(576, D), buf(3, 576, 384), buf(8, 72, 384),
        buf(7, 72, 384), buf(72, 384), buf(7, 72, 384), buf(72, 384), buf(4, 72, 384),
        pltpu.SemaphoreType.DMA((N_MSG, 16)), pltpu.SemaphoreType.DMA((N_MSG, 16)),
        pltpu.SemaphoreType.DMA((15,)), pltpu.SemaphoreType.DMA((16,)),
        pltpu.SemaphoreType.DMA((4,)), pltpu.SemaphoreType.DMA((4,)),
        pltpu.SemaphoreType.DMA((40,)), pltpu.SemaphoreType.DMA((40,)),
    ]
    out = jax.ShapeDtypeStruct((20, 8, D), BF)
    results = pl.pallas_call(
        kernel,
        out_shape=[out] * 6 + [jax.ShapeDtypeStruct((72, D), F32)],
        in_specs=[vm] * 8,
        out_specs=[vm] * 7,
        scratch_shapes=scratch,
        compiler_params=pltpu.CompilerParams(
            collective_id=0, has_side_effects=True, vmem_limit_bytes=56 * 1024 * 1024
        ),
        name="step",
    )(*flat[:6], weight, flat[6])
    return tuple(item.reshape(q_space.shape) for item in results[:6]) + (results[6],)


def solution(mesh):
    token = P("dp", "seq", None)
    return jax.shard_map(
        shards,
        mesh=mesh,
        in_specs=(token,) * 6 + (P("dp", None), token),
        out_specs=(token,) * 6 + (P("seq", None),),
        check_vma=False,
    )
```

```python
import functools
import math

import jax
import jax.numpy as jnp
from jax import lax
from jax.experimental import pallas as pl
from jax.experimental.pallas import tpu as pltpu
from jax.sharding import PartitionSpec as P

HEADS = 16
HEAD_DIM = 72
D = 1152
TOK = 160
MAIN = 128
SCALING = 1.0 / math.sqrt(HEAD_DIM)
BF = jnp.bfloat16
F32 = jnp.float32
MESH = pl.DeviceIdType.MESH
MQ, MTQ, MA, MTA, MO, MTO, MG, MTG = 0, 9, 10, 11, 12, 15, 16, 25
N_MSG = 26


def dot_nn(a, b):
    return lax.dot_general(a, b, (((1,), (0,)), ((), ())), preferred_element_type=F32)


def dot_nt(a, b):
    return lax.dot_general(a, b, (((1,), (1,)), ((), ())), preferred_element_type=F32)


def dot_tn(a, b):
    return lax.dot_general(a, b, (((0,), (0,)), ((), ())), preferred_element_type=F32)


def window(head, last=7):
    start = jnp.minimum((9 * head) // 16, last) * 128
    lanes = lax.broadcasted_iota(jnp.int32, (1, 256), 1) + start
    inside = jnp.logical_and(lanes >= HEAD_DIM * head, lanes < HEAD_DIM * head + HEAD_DIM)
    return pl.ds(pl.multiple_of(start, 128), 256), inside


def get(ref, cols):
    value = ref[:, :, cols]
    return value.reshape(8 * ref.shape[0], value.shape[2])


def put(ref, cols, value):
    ref[:, :, cols] = value.astype(BF).reshape(ref.shape[0], 8, value.shape[1])


def put_head(ref, cols, inside, value):
    put(ref, cols, jnp.where(inside, value, get(ref, cols).astype(F32)))


def forward_head(head, q_ref, k_ref, v_ref, bias_ref, probs_ref, out_ref, last=7):
    cols, inside = window(head, last)
    chosen = inside.astype(F32).astype(BF)
    logits = dot_nt(get(q_ref, cols) * chosen, get(k_ref, cols)) * SCALING
    if bias_ref is not None:
        logits = logits + bias_ref[...]
    lifted = jnp.exp(logits - jnp.max(logits, axis=-1, keepdims=True))
    probs = lifted * (1.0 / jnp.sum(lifted, axis=-1, keepdims=True))
    probs_ref[head] = probs
    put_head(out_ref, cols, inside, dot_nn(probs.astype(BF), get(v_ref, cols)))


def backward_head(head, q_ref, k_ref, v_ref, probs_ref, step_ref, gq_ref, gk_ref, gv_ref):
    cols, inside = window(head)
    chosen = inside.astype(F32).astype(BF)
    step = get(step_ref, cols)
    probs = probs_ref[head]
    upstream = dot_nt(step * chosen, get(v_ref, cols))
    put_head(gv_ref, cols, inside, dot_tn(probs.astype(BF), step))
    scores = (probs * (upstream - jnp.sum(probs * upstream, axis=-1, keepdims=True))).astype(BF)
    put_head(gq_ref, cols, inside, dot_nn(scores, get(k_ref, cols)) * SCALING)
    put_head(gk_ref, cols, inside, dot_tn(scores, get(q_ref, cols)) * SCALING)


def for_heads(first, last, step):
    def pair(i, carry):
        step(first + 2 * i)
        step(first + 2 * i + 1)
        return carry

    lax.fori_loop(0, (last - first) // 2, pair, 0)
    if (last - first) % 2:
        step(last - 1)


def iota(shape, axis):
    return lax.broadcasted_iota(jnp.int32, shape, axis)


def kernel(
    qs_in, ks_in, vs_in, qt_in, kt_in, vt_in, w_in, target_in,
    gqs, gks, gvs, rgq_out, rgk_out, rgv_out, rtg_out, sums,
    qs, ks, vs, qt, kt, vt, w_own, target, wb, w, rq, rk, rv, ra, rtq, rta, tq, ta, to, tg, space, over, step_b, step_f,
    ot, ro, rto, comb, gradp, gradt, gq, gk, gv, rgq, rgk, rgv, rtg, probs_s, probs_t, bias,
    wgp, r1, half, r2, r2n, h2, n2, r3, r3n, h3, h3n, r4, r4n, h4, h4n, r5, r5n,
    isem, ssem, rsem, wsend, wrecv, csend, crecv, rsend, rrecv,
):
    dp = lax.axis_index("dp")
    s = lax.axis_index("seq")
    core = lax.rem(dp, 2)
    chip = dp // 2
    x = chip // 4
    zl = lax.rem(chip, 4)
    zh = s // 8
    y = lax.rem(s, 8)

    def device(x_, zl_, core_, zh_, y_):
        return ((x_ * 4 + zl_) * 2 + core_, zh_ * 8 + y_)

    def plus(value, k, n):
        return lax.rem(value + k, n)

    def along_z(k):
        z_ = lax.rem(zh * 4 + zl + k, 8)
        return device(x, lax.rem(z_, 4), core, z_ // 4, y)

    sibling = device(x, zl, 1 - core, zh, y)

    loads = [
        pltpu.make_async_copy(src, dst, isem.at[n])
        for n, (src, dst) in enumerate(
            ((qt_in, qt), (kt_in, kt), (vt_in, vt), (w_in, w_own), (qs_in, qs), (ks_in, ks),
             (vs_in, vs), (target_in, target))
        )
    ]
    for load in loads:
        load.start()

    barrier = pltpu.get_barrier_semaphore()

    def greet(who):
        pl.semaphore_signal(barrier, inc=1, device_id=who, device_id_type=MESH)

    for k in range(1, 16):
        greet((dp, plus(s, k, 16)))
    for k in range(1, 4):
        greet(device(x, plus(zl, k, 4), core, zh, y))
        greet(device(x, plus(zl, k, 4), core, 1 - zh, y))
        greet(device(plus(x, k, 4), zl, core, zh, y))
        greet(device(plus(x, k, 4), zl, 1 - core, zh, y))
    greet(sibling)

    def to_peer(msg, src, dst, peer, cols=None):
        a, b = src.at[peer], dst.at[s]
        if cols is not None:
            a, b = src.at[peer, :, cols], dst.at[s, :, cols]
        return pltpu.make_async_remote_copy(
            src_ref=a, dst_ref=b, send_sem=ssem.at[msg, peer], recv_sem=rsem.at[msg, s],
            device_id=(dp, peer), device_id_type=MESH,
        )

    def from_peer(msg, src, dst, peer, cols=None):
        a, b = src.at[peer], dst.at[peer]
        if cols is not None:
            a, b = src.at[peer, :, cols], dst.at[peer, :, cols]
        return pltpu.make_async_remote_copy(
            src_ref=a, dst_ref=b, send_sem=ssem.at[msg, peer], recv_sem=rsem.at[msg, peer],
            device_id=(dp, peer), device_id_type=MESH,
        )

    def turn(n):
        return lax.rem((lax.rem(n, 2) * (n + 1) + (1 - lax.rem(n, 2)) * (16 - n)) // 2, 8)

    def send_to(items, peer):
        for msg, src, dst, cols in items:
            to_peer(msg, src, dst, peer, cols).start()

    def send_near(items, n):
        send_to(items, zh * 8 + plus(y, turn(n), 8))

    def send_far(items, n):
        send_to(items, (1 - zh) * 8 + plus(y, turn(n), 8))

    def keep_own(items):
        for msg, src, dst, cols in items:
            if cols is None:
                dst[s] = src[s]
            else:
                dst[s, :, cols] = src[s, :, cols]

    def scatter_near(items):
        lax.fori_loop(1, 8, lambda n, carry: (send_near(items, n), carry)[1], 0)

    def scatter_far(items):
        lax.fori_loop(0, 8, lambda n, carry: (send_far(items, n), carry)[1], 0)
        keep_own(items)

    def scatter(items):
        def one(n, carry):
            send_far(items, n)
            send_near(items, n)
            return carry

        send_far(items, 0)
        lax.fori_loop(1, 8, one, 0)
        keep_own(items)

    def gathered(items):
        def one(k, carry):
            peer = plus(s, k, 16)
            for msg, src, dst, cols in items:
                from_peer(msg, src, dst, peer, cols).wait_recv()
            return carry

        lax.fori_loop(1, 16, one, 0)

    def drained(items):
        def one(k, carry):
            peer = plus(s, k, 16)
            for msg, src, dst, cols in items:
                to_peer(msg, src, dst, peer, cols).wait_send()
            return carry

        lax.fori_loop(1, 16, one, 0)

    thirds = [pl.ds(384 * c, 384) for c in range(3)]
    qkv_items = [
        [
            (MQ + 3 * c, qt, rq, thirds[c]),
            (MQ + 3 * c + 1, kt, rk, thirds[c]),
            (MQ + 3 * c + 2, vt, rv, thirds[c]),
        ]
        for c in range(3)
    ]
    tq_items = [(MTQ, tq, rtq, None)]
    a_items = [(MA, over, ra, None), (MTA, ta, rta, None)]
    o_items = [[(MO + c, ot, ro, thirds[c])] for c in range(3)]
    to_items = [(MTO, to, rto, None)]
    g_items = [
        [
            (MG + 3 * c, gq, rgq, thirds[c]),
            (MG + 3 * c + 1, gk, rgk, thirds[c]),
            (MG + 3 * c + 2, gv, rgv, thirds[c]),
        ]
        for c in range(3)
    ]
    tg_items = [(MTG, tg, rtg, None)]

    def w_copy(src, slot, k, who):
        return pltpu.make_async_remote_copy(
            src_ref=src, dst_ref=wb.at[core, slot], send_sem=wsend.at[k], recv_sem=wrecv.at[slot],
            device_id=who, device_id_type=MESH,
        )

    def w_start():
        for n, k in enumerate((1, 7, 2 + 4 * core)):
            w_copy(w_own, chip, n, along_z(k)).start()
        for k in range(1, 4):
            w_copy(w_own, chip, 2 + k, device(plus(x, k, 4), zl, core, zh, y)).start()
        wb[core, chip] = w_own[...]

    def w_core(group):
        part = wb.at[core, pl.ds(4 * group, 4)]
        return pltpu.make_async_remote_copy(
            src_ref=part, dst_ref=part, send_sem=csend.at[group], recv_sem=crecv.at[group],
            device_id=sibling, device_id_type=MESH,
        )

    def w_other(group):
        part = wb.at[1 - core, pl.ds(4 * group, 4)]
        return pltpu.make_async_remote_copy(
            src_ref=part, dst_ref=part, send_sem=csend.at[group], recv_sem=crecv.at[group],
            device_id=sibling, device_id_type=MESH,
        )

    def w_forward():
        for j in range(1, 4):
            slot = x * 4 + plus(zl, j, 4)
            part = wb.at[core, slot]
            w_copy(part, slot, 0, sibling).wait_recv()
            for k in range(1, 4):
                who = device(plus(x, k, 4), zl, core, zh, y)
                w_copy(part, slot, 3 * j + 2 + k, who).start()
        w_core(x).start()

    def w_share():
        for k in range(1, 4):
            group = plus(x, k, 4)
            for j in range(4):
                slot = group * 4 + j
                w_copy(wb.at[core, slot], slot, 0, sibling).wait_recv()
            w_core(group).start()

    def w_finish():
        for group in range(4):
            w_other(group).wait_recv()

        def lay(i, carry):
            slots = [wb[0, 2 * i], wb[1, 2 * i], wb[0, 2 * i + 1], wb[1, 2 * i + 1]]
            w[pl.ds(pl.multiple_of(144 * i, 16), 144), :] = jnp.concatenate(slots, axis=0)
            return carry

        lax.fori_loop(0, 8, lay, 0)

    def w_drained():
        for k in range(6):
            w_copy(w_own, chip, k, sibling).wait_send()
        for k in range(6, 15):
            w_copy(w_own, chip, k, sibling).wait_send()
        for group in range(4):
            w_core(group).wait_send()

    def packer():
        i, m = iota((128, 96), 0), iota((128, 96), 1)
        r = lax.rem(i, 8)
        source = 32 * (r // 2) + 2 * (i // 8) + lax.rem(r, 2)
        return jnp.where(jnp.logical_and(m == source, r < 6), 1.0, 0.0).astype(BF)

    def unpacker(k):
        i, m = iota((32, 128), 0), iota((32, 128), 1)
        return jnp.where(m == 8 * (i // 2) + 2 * k + lax.rem(i, 2), 1.0, 0.0).astype(BF)

    every = pl.ds(0, D)

    def last_rows(part, cols):
        value = part[16:20, :, cols]
        return value.reshape(32, value.shape[2])

    def whole(ref):
        return ref[...].reshape(128, ref.shape[2])

    def pack(stack, dst):
        dst[...] = dot_nn(packer(), stack).astype(BF).reshape(dst.shape)

    def unpack(src, k, part, cols):
        part[16:20, :, cols] = dot_nn(unpacker(k), whole(src)).astype(BF).reshape(4, 8, src.shape[2])

    def pack_arrays(parts, dst):
        pack(jnp.concatenate([last_rows(p, every) for p in parts], axis=0), dst)

    def unpack_arrays(src, parts):
        for k, part in enumerate(parts):
            unpack(src, k, part, every)

    def pack_thirds(part, dst):
        pack(jnp.concatenate([last_rows(part, thirds[g]) for g in range(3)], axis=0), dst)

    def unpack_thirds(src, part):
        for g in range(3):
            unpack(src, g, part, thirds[g])

    def in_thirds(step):
        def one(c, carry):
            step(pl.ds(pl.multiple_of(384 * c, 128), 384))
            return carry

        lax.fori_loop(0, 3, one, 0)

    i, m = iota((TOK, TOK), 0), iota((TOK, TOK), 1)
    patch_i = jnp.where(i < MAIN, lax.rem(i, 8), 8 + lax.rem(i, 2))
    patch_m = jnp.where(m < MAIN, lax.rem(m, 8), 8 + lax.rem(m, 2))
    bias[...] = jnp.where(patch_i == patch_m, 0.0, -1e30)
    for load in loads[:4]:
        load.wait()
    pack_arrays([qt, kt, vt], tq)
    pl.semaphore_wait(barrier, 28)
    w_start()
    scatter_near(tq_items)
    for c in range(3):
        scatter_near(qkv_items[c])
    for load in loads[4:]:
        load.wait()

    def space_forward(h):
        forward_head(h, qs, ks, vs, None, probs_s, space)

    for_heads(0, 8, space_forward)
    w_forward()
    scatter_far(tq_items)
    for c in range(3):
        scatter_far(qkv_items[c])
    for_heads(8, 16, space_forward)
    w_share()
    w_finish()

    def project_space(cols):
        product = dot_nn(get(space, every), w[:, cols])
        put(gradp, cols, product - get(target, cols).astype(F32))

    in_thirds(project_space)

    def back_space(cols):
        put(over, cols, dot_nt(get(gradp, every), w[cols, :]))

    in_thirds(back_space)
    pack_thirds(over, ta)

    gathered(tq_items)
    unpack_arrays(rtq, [rq, rk, rv])

    def time_forward(last):
        return lambda h: forward_head(h, rq, rk, rv, bias, probs_t, ot, last)

    gathered(qkv_items[0])
    for_heads(0, 5, time_forward(1))
    gathered(qkv_items[1])
    for_heads(5, 10, time_forward(4))
    scatter(o_items[0])
    gathered(qkv_items[2])
    for_heads(10, 12, time_forward(7))
    scatter(o_items[1])
    for_heads(12, 16, time_forward(7))
    pack_thirds(ot, to)
    scatter(o_items[2] + to_items)
    scatter(a_items)

    def project_time(cols):
        put(gradt, cols, dot_nn(get(ot, every), w[:, cols]))

    def back_time(cols):
        share = dot_nt(get(gradt, every), w[cols, :])
        put(step_b, cols, share + get(ra, cols).astype(F32))

    def time_backward(h):
        backward_head(h, rq, rk, rv, probs_t, step_b, gq, gk, gv)

    def send_grads(c):
        scatter(g_items[c])

    gathered(to_items)
    for c in range(3):
        gathered(o_items[c])
    unpack_thirds(rto, ro)
    comb[...] = (space[...].astype(F32) + ro[...].astype(F32)).astype(BF)

    def project_all(cols):
        product = dot_nn(get(comb, every), w[:, cols])
        put(gradp, cols, product - get(target, cols).astype(F32))

    in_thirds(project_all)

    def to_sibling(j):
        rows = pl.ds(pl.multiple_of(576 * (1 - core) + 144 * j, 16), 144)
        return pltpu.make_async_remote_copy(
            src_ref=wgp.at[rows], dst_ref=r1.at[pl.ds(144 * j, 144)],
            send_sem=rsend.at[j], recv_sem=rrecv.at[j], device_id=sibling, device_id_type=MESH,
        )

    def x_window(x_):
        return pl.ds(pl.multiple_of(256 * x_, 128), 256)

    ninth = pl.ds(1024, 128)

    def to_x(j, k):
        x_ = plus(x, k, 4)
        rows = pl.ds(144 * j, 144)
        return pltpu.make_async_remote_copy(
            src_ref=half.at[rows, x_window(x_)], dst_ref=r2.at[k - 1, rows],
            send_sem=rsend.at[4 + 3 * j + k - 1], recv_sem=rrecv.at[4 + 3 * j + k - 1],
            device_id=device(x_, zl, core, zh, y), device_id_type=MESH,
        )

    def to_x_ninth(k):
        x_ = plus(x, k, 4)
        return pltpu.make_async_remote_copy(
            src_ref=half.at[pl.ds(pl.multiple_of(144 * x_, 16), 144), ninth], dst_ref=r2n.at[k - 1],
            send_sem=rsend.at[39 + k], recv_sem=rrecv.at[39 + k],
            device_id=device(x_, zl, core, zh, y), device_id_type=MESH,
        )

    def to_y(k):
        y_ = plus(y, k, 8)
        return pltpu.make_async_remote_copy(
            src_ref=h2.at[y_], dst_ref=r3.at[k - 1],
            send_sem=rsend.at[15 + k], recv_sem=rrecv.at[15 + k],
            device_id=device(x, zl, core, zh, y_), device_id_type=MESH,
        )

    def to_y_ninth(n):
        y_ = 2 * x + n
        slot = plus(y, 15 - y_, 8)
        return pltpu.make_async_remote_copy(
            src_ref=n2.at[n], dst_ref=r3n.at[slot], send_sem=rsend.at[43 + n],
            recv_sem=rrecv.at[45 + slot], device_id=device(x, zl, core, zh, y_), device_id_type=MESH,
        )

    def from_y_ninth(slot):
        return pltpu.make_async_remote_copy(
            src_ref=n2.at[0], dst_ref=r3n.at[slot], send_sem=rsend.at[43],
            recv_sem=rrecv.at[45 + slot], device_id=sibling, device_id_type=MESH,
        )

    def to_z(k, same, ninth_=False):
        zh_ = zh if same else 1 - zh
        slot = k - 1 if same else 3 + k
        src, dst, sem = (h3n, r4n, 52) if ninth_ else (h3, r4, 23)
        return pltpu.make_async_remote_copy(
            src_ref=src, dst_ref=dst.at[slot], send_sem=rsend.at[sem + slot],
            recv_sem=rrecv.at[sem + slot], device_id=device(x, plus(zl, k, 4), core, zh_, y),
            device_id_type=MESH,
        )

    def final_peer(k, flip):
        return device(plus(x, k, 4), zl, core if flip == 0 else 1 - core, zh, y)

    def to_all(k, flip):
        slot = k - 1 if flip == 0 else 3 + k
        return pltpu.make_async_remote_copy(
            src_ref=h4, dst_ref=r5.at[x], send_sem=rsend.at[31 + slot], recv_sem=rrecv.at[31 + x],
            device_id=final_peer(k, flip), device_id_type=MESH,
        )

    def to_all_ninth(k, flip):
        slot = k - 1 if flip == 0 else 3 + k
        return pltpu.make_async_remote_copy(
            src_ref=h4n, dst_ref=r5n, send_sem=rsend.at[59 + slot], recv_sem=rrecv.at[59],
            device_id=final_peer(k, flip), device_id_type=MESH,
        )

    def from_all(x_):
        return pltpu.make_async_remote_copy(
            src_ref=h4, dst_ref=r5.at[x_], send_sem=rsend.at[31], recv_sem=rrecv.at[31 + x_],
            device_id=sibling, device_id_type=MESH,
        )

    everyone = [(k, 0) for k in range(1, 4)] + [(k, 1) for k in range(4)]
    around_z = [(k, True) for k in range(1, 4)] + [(k, False) for k in range(4)]
    here = zh == core
    owner = y // 2 == x

    def terms(i, carry):
        j = core * i + (1 - core) * (8 - i)
        rows = pl.ds(pl.multiple_of(128 * j, 128), 128)
        wgp[rows, :] = dot_tn(get(comb, rows), get(gradp, every)).astype(BF)
        return carry

    def back_all(cols):
        put(step_f, cols, dot_nt(get(gradp, every), w[cols, :]))

    lax.fori_loop(0, 5, terms, 0)
    for j in range(4):
        to_sibling(j).start()
    lax.fori_loop(5, 9, terms, 0)
    in_thirds(back_all)

    in_thirds(project_time)
    gathered(a_items)
    unpack_thirds(rta, ra)
    in_thirds(back_time)
    for_heads(0, 6, time_backward)
    send_grads(0)

    for j in range(4):
        to_sibling(j).wait_recv()
        rows = pl.ds(144 * j, 144)
        own = wgp[pl.ds(pl.multiple_of(576 * core + 144 * j, 16), 144), :]
        half[rows, :] = (own.astype(F32) + r1[rows, :].astype(F32)).astype(BF)
        for k in range(1, 4):
            to_x(j, k).start()

    for k in range(1, 4):
        to_x_ninth(k).start()
    for_heads(6, 12, time_backward)
    send_grads(1)
    for_heads(12, 16, time_backward)
    send_grads(2)
    pack_arrays([gq, gk, gv], tg)
    scatter(tg_items)

    def space_backward(h):
        backward_head(h, qs, ks, vs, probs_s, step_f, gqs, gks, gvs)

    for_heads(0, 16, space_backward)

    for j in range(4):
        for k in range(1, 4):
            to_x(j, k).wait_recv()
        for i in range(2):
            rows = pl.ds(144 * j + 72 * i, 72)
            total = half[rows, x_window(x)].astype(F32)
            for k in range(1, 4):
                total = total + r2[k - 1, rows, :].astype(F32)
            h2[2 * j + i] = total.astype(BF)
    for k in (1, 7, 2, 6, 3, 5, 4):
        to_y(k).start()
    total = half[pl.ds(pl.multiple_of(144 * x, 16), 144), ninth].astype(F32)
    for k in range(1, 4):
        to_x_ninth(k).wait_recv()
        total = total + r2n[k - 1].astype(F32)
    n2[...] = total.astype(BF).reshape(2, 72, 128)
    for n in range(2):

        @pl.when(y != 2 * x + n)
        def _(n=n):
            to_y_ninth(n).start()

    drained(qkv_items[0] + qkv_items[1] + qkv_items[2])
    drained(tq_items + a_items + to_items + o_items[0] + o_items[1] + o_items[2])
    drained(g_items[0] + g_items[1])
    w_drained()

    total = h2[y].astype(F32)
    for k in range(1, 8):
        to_y(k).wait_recv()
        total = total + r3[k - 1].astype(F32)
    h3[...] = total.astype(BF)

    @pl.when(here)
    def _():
        for k in range(1, 4):
            to_z(k, True).start()

    @pl.when(jnp.logical_not(here))
    def _():
        for k in range(4):
            to_z(k, False).start()

    @pl.when(owner)
    def _():
        total = n2[lax.rem(y, 2)].astype(F32)
        for slot in range(7):
            from_y_ninth(slot).wait_recv()
            total = total + r3n[slot].astype(F32)
        h3n[...] = total.astype(BF)

        @pl.when(here)
        def _():
            for k in range(1, 4):
                to_z(k, True, True).start()

        @pl.when(jnp.logical_not(here))
        def _():
            for k in range(4):
                to_z(k, False, True).start()

    @pl.when(here)
    def _():
        total = h3[...].astype(F32)
        for n, (k, same) in enumerate(around_z):
            to_z(k, same).wait_recv()
            total = total + r4[n].astype(F32)
        h4[...] = total.astype(BF)
        for k, flip in everyone:
            to_all(k, flip).start()
        r5[x] = h4[...]

        @pl.when(owner)
        def _():
            total = h3n[...].astype(F32)
            for n, (k, same) in enumerate(around_z):
                to_z(k, same, True).wait_recv()
                total = total + r4n[n].astype(F32)
            h4n[...] = total.astype(BF)
            for k, flip in everyone:
                to_all_ninth(k, flip).start()
            r5n[...] = h4n[...]

        @pl.when(jnp.logical_not(owner))
        def _():
            to_all_ninth(0, 1).wait_recv()

        for k in range(1, 4):
            from_all(plus(x, k, 4)).wait_recv()
        for k in range(1, 4):
            to_z(k, True).wait_send()
        for k, flip in everyone:
            to_all(k, flip).wait_send()

        @pl.when(owner)
        def _():
            for k in range(1, 4):
                to_z(k, True, True).wait_send()
            for k, flip in everyone:
                to_all_ninth(k, flip).wait_send()

    @pl.when(jnp.logical_not(here))
    def _():
        for k in range(4):
            from_all(plus(x, k, 4)).wait_recv()
        to_all_ninth(0, 1).wait_recv()
        for k in range(4):
            to_z(k, False).wait_send()

        @pl.when(owner)
        def _():
            for k in range(4):
                to_z(k, False, True).wait_send()

    for c in range(4):
        sums[:, pl.ds(256 * c, 256)] = r5[c]
    sums[:, ninth] = r5n[...]

    for c in range(3):
        gathered(g_items[c])
    gathered(tg_items)
    for src, dst in ((rgq, rgq_out), (rgk, rgk_out), (rgv, rgv_out), (rtg, rtg_out)):
        dst[...] = src[...]

    drained(g_items[2] + tg_items)
    for j in range(4):
        to_sibling(j).wait_send()
        for k in range(1, 4):
            to_x(j, k).wait_send()
    for k in range(1, 4):
        to_x_ninth(k).wait_send()
    for k in range(1, 8):
        to_y(k).wait_send()
    for n in range(2):

        @pl.when(y != 2 * x + n)
        def _(n=n):
            to_y_ninth(n).wait_send()


def finish(gqs, gks, gvs, rgq, rgk, rgv, rtg, sums, *out):
    for src, dst in zip((gqs, gks, gvs), out[:3]):
        dst[...] = src[...]
    packed = rtg[...].reshape(128, D)
    for k, (src, dst) in enumerate(zip((rgq, rgk, rgv), out[3:6])):
        i, m = iota((32, 128), 0), iota((32, 128), 1)
        chosen = jnp.where(m == 8 * (i // 2) + 2 * k + lax.rem(i, 2), 1.0, 0.0).astype(BF)
        dst[0:16] = src[...]
        dst[16:20] = dot_nn(chosen, packed).astype(BF).reshape(4, 8, D)
    out[6][...] = sums[...].astype(F32) * (1.0 / math.sqrt(81920))


def shards(q_space, k_space, v_space, q_time, k_time, v_time, weight, target):
    tokens = (q_space, k_space, v_space, q_time, k_time, v_time, target)
    flat = [item.reshape(20, 8, D) for item in tokens]
    vm = pl.BlockSpec(memory_space=pltpu.VMEM)
    anywhere = pl.BlockSpec(memory_space=pltpu.HBM)

    def buf(*shape, dtype=BF):
        return pltpu.VMEM(shape, dtype)

    tok = buf(20, 8, D)
    main = buf(16, 8, D)
    third = buf(16, 8, 384)
    scratch = [
        tok, tok, tok, tok, tok, tok, buf(36, D), tok,
        buf(2, 16, 36, D), buf(D, D),
        tok, tok, tok, tok,
        main, third, main, third, third, main,
        tok, tok, tok, tok,
        tok, tok, third, tok, tok, tok,
        tok, tok, tok, main, main, main, main,
        buf(HEADS, TOK, TOK, dtype=F32), buf(HEADS, TOK, TOK, dtype=F32), buf(TOK, TOK, dtype=F32),
        buf(D, D), buf(576, D), buf(576, D), buf(3, 576, 256), buf(3, 144, 128),
        buf(8, 72, 256), buf(2, 72, 128), buf(7, 72, 256), buf(7, 72, 128),
        buf(72, 256), buf(72, 128), buf(7, 72, 256), buf(7, 72, 128),
        buf(72, 256), buf(72, 128), buf(4, 72, 256), buf(72, 128),
        pltpu.SemaphoreType.DMA((8,)),
        pltpu.SemaphoreType.DMA((N_MSG, 16)), pltpu.SemaphoreType.DMA((N_MSG, 16)),
        pltpu.SemaphoreType.DMA((15,)), pltpu.SemaphoreType.DMA((16,)),
        pltpu.SemaphoreType.DMA((4,)), pltpu.SemaphoreType.DMA((4,)),
        pltpu.SemaphoreType.DMA((68,)), pltpu.SemaphoreType.DMA((68,)),
    ]
    out = jax.ShapeDtypeStruct((20, 8, D), BF)
    part = jax.ShapeDtypeStruct((16, 8, D), BF)
    middle = pl.pallas_call(
        kernel,
        out_shape=[out] * 3 + [part] * 4 + [jax.ShapeDtypeStruct((72, D), BF)],
        in_specs=[anywhere] * 8,
        out_specs=[vm] * 8,
        scratch_shapes=scratch,
        compiler_params=pltpu.CompilerParams(
            collective_id=0, has_side_effects=True, vmem_limit_bytes=56 * 1024 * 1024
        ),
        name="step",
    )(*flat[:6], weight, flat[6])
    results = pl.pallas_call(
        finish,
        out_shape=[out] * 6 + [jax.ShapeDtypeStruct((72, D), F32)],
        in_specs=[vm] * 8,
        out_specs=[vm] * 7,
        compiler_params=pltpu.CompilerParams(vmem_limit_bytes=60 * 1024 * 1024),
        name="finish",
    )(*middle)
    return tuple(item.reshape(q_space.shape) for item in results[:6]) + (results[6],)


def solution(mesh):
    token = P("dp", "seq", None)
    return jax.shard_map(
        shards,
        mesh=mesh,
        in_specs=(token,) * 6 + (P("dp", None), token),
        out_specs=(token,) * 6 + (P("seq", None),),
        check_vma=False,
    )
```

```python
import functools
import math

import jax
import jax.numpy as jnp
from jax import lax
from jax.experimental import pallas as pl
from jax.experimental.pallas import tpu as pltpu
from jax.sharding import PartitionSpec as P

HEADS = 16
HEAD_DIM = 72
D = 1152
TOK = 160
MAIN = 128
SCALING = 1.0 / math.sqrt(HEAD_DIM)
BF = jnp.bfloat16
F32 = jnp.float32
MESH = pl.DeviceIdType.MESH
MQ, MTQ, MA, MTA, MO, MTO, MG, MTG = 0, 9, 10, 11, 12, 15, 16, 25
N_MSG = 26


def dot_nn(a, b):
    return lax.dot_general(a, b, (((1,), (0,)), ((), ())), preferred_element_type=F32)


def dot_nt(a, b):
    return lax.dot_general(a, b, (((1,), (1,)), ((), ())), preferred_element_type=F32)


def dot_tn(a, b):
    return lax.dot_general(a, b, (((0,), (0,)), ((), ())), preferred_element_type=F32)


def window(head, last=7):
    start = jnp.minimum((9 * head) // 16, last) * 128
    lanes = lax.broadcasted_iota(jnp.int32, (1, 256), 1) + start
    inside = jnp.logical_and(lanes >= HEAD_DIM * head, lanes < HEAD_DIM * head + HEAD_DIM)
    return pl.ds(pl.multiple_of(start, 128), 256), inside


def get(ref, cols):
    value = ref[:, :, cols]
    return value.reshape(8 * ref.shape[0], value.shape[2])


def put(ref, cols, value):
    ref[:, :, cols] = value.astype(BF).reshape(ref.shape[0], 8, value.shape[1])


def put_head(ref, cols, inside, value):
    put(ref, cols, jnp.where(inside, value, get(ref, cols).astype(F32)))


def forward_head(head, q_ref, k_ref, v_ref, bias_ref, probs_ref, out_ref, last=7):
    cols, inside = window(head, last)
    chosen = inside.astype(F32).astype(BF)
    logits = dot_nt(get(q_ref, cols) * chosen, get(k_ref, cols)) * SCALING
    if bias_ref is not None:
        logits = logits + bias_ref[...]
    lifted = jnp.exp(logits - jnp.max(logits, axis=-1, keepdims=True))
    probs = lifted * (1.0 / jnp.sum(lifted, axis=-1, keepdims=True))
    probs_ref[head] = probs
    put_head(out_ref, cols, inside, dot_nn(probs.astype(BF), get(v_ref, cols)))


def backward_head(head, q_ref, k_ref, v_ref, probs_ref, step_ref, gq_ref, gk_ref, gv_ref):
    cols, inside = window(head)
    chosen = inside.astype(F32).astype(BF)
    step = get(step_ref, cols)
    probs = probs_ref[head]
    upstream = dot_nt(step * chosen, get(v_ref, cols))
    put_head(gv_ref, cols, inside, dot_tn(probs.astype(BF), step))
    scores = (probs * (upstream - jnp.sum(probs * upstream, axis=-1, keepdims=True))).astype(BF)
    put_head(gq_ref, cols, inside, dot_nn(scores, get(k_ref, cols)) * SCALING)
    put_head(gk_ref, cols, inside, dot_tn(scores, get(q_ref, cols)) * SCALING)


def for_heads(first, last, step):
    def pair(i, carry):
        step(first + 2 * i)
        step(first + 2 * i + 1)
        return carry

    lax.fori_loop(0, (last - first) // 2, pair, 0)
    if (last - first) % 2:
        step(last - 1)


def iota(shape, axis):
    return lax.broadcasted_iota(jnp.int32, shape, axis)


def kernel(
    qs_in, ks_in, vs_in, qt_in, kt_in, vt_in, w_in, target_in,
    gqs, gks, gvs, rgq_out, rgk_out, rgv_out, rtg_out, sums,
    qs, ks, vs, qt, kt, vt, w_own, target, wb, w, rq, rk, rv, ra, rtq, rta, tq, ta, to, tg, space, over, step_b, step_f,
    ot, ro, rto, comb, gradp, gradt, gq, gk, gv, rgq, rgk, rgv, rtg, probs_s, probs_t, bias,
    wgp, r1, half, r2, r2n, h2, n2, r3, r3n, h3, h3n, r4, r4n, h4, h4n, r5, r5n,
    isem, ssem, rsem, wsend, wrecv, csend, crecv, rsend, rrecv,
):
    dp = lax.axis_index("dp")
    s = lax.axis_index("seq")
    core = lax.rem(dp, 2)
    chip = dp // 2
    x = chip // 4
    zl = lax.rem(chip, 4)
    zh = s // 8
    y = lax.rem(s, 8)

    def device(x_, zl_, core_, zh_, y_):
        return ((x_ * 4 + zl_) * 2 + core_, zh_ * 8 + y_)

    def plus(value, k, n):
        return lax.rem(value + k, n)

    def along_z(k):
        z_ = lax.rem(zh * 4 + zl + k, 8)
        return device(x, lax.rem(z_, 4), core, z_ // 4, y)

    sibling = device(x, zl, 1 - core, zh, y)

    loads = [
        pltpu.make_async_copy(src, dst, isem.at[n])
        for n, (src, dst) in enumerate(
            ((qt_in, qt), (kt_in, kt), (vt_in, vt), (w_in, w_own), (qs_in, qs), (ks_in, ks),
             (vs_in, vs), (target_in, target))
        )
    ]
    for load in loads:
        load.start()

    barrier = pltpu.get_barrier_semaphore()

    def greet(who):
        pl.semaphore_signal(barrier, inc=1, device_id=who, device_id_type=MESH)

    for k in range(1, 16):
        greet((dp, plus(s, k, 16)))
    for k in range(1, 4):
        greet(device(x, plus(zl, k, 4), core, zh, y))
        greet(device(x, plus(zl, k, 4), core, 1 - zh, y))
        greet(device(plus(x, k, 4), zl, core, zh, y))
        greet(device(plus(x, k, 4), zl, 1 - core, zh, y))
    greet(sibling)

    def to_peer(msg, src, dst, peer, cols=None):
        a, b = src.at[peer], dst.at[s]
        if cols is not None:
            a, b = src.at[peer, :, cols], dst.at[s, :, cols]
        return pltpu.make_async_remote_copy(
            src_ref=a, dst_ref=b, send_sem=ssem.at[msg, peer], recv_sem=rsem.at[msg, s],
            device_id=(dp, peer), device_id_type=MESH,
        )

    def from_peer(msg, src, dst, peer, cols=None):
        a, b = src.at[peer], dst.at[peer]
        if cols is not None:
            a, b = src.at[peer, :, cols], dst.at[peer, :, cols]
        return pltpu.make_async_remote_copy(
            src_ref=a, dst_ref=b, send_sem=ssem.at[msg, peer], recv_sem=rsem.at[msg, peer],
            device_id=(dp, peer), device_id_type=MESH,
        )

    def turn(n):
        return lax.rem((lax.rem(n, 2) * (n + 1) + (1 - lax.rem(n, 2)) * (16 - n)) // 2, 8)

    def send_to(items, peer):
        for msg, src, dst, cols in items:
            to_peer(msg, src, dst, peer, cols).start()

    def send_near(items, n):
        send_to(items, zh * 8 + plus(y, turn(n), 8))

    def send_far(items, n):
        send_to(items, (1 - zh) * 8 + plus(y, turn(n), 8))

    def keep_own(items):
        for msg, src, dst, cols in items:
            if cols is None:
                dst[s] = src[s]
            else:
                dst[s, :, cols] = src[s, :, cols]

    def scatter_near(items):
        lax.fori_loop(1, 8, lambda n, carry: (send_near(items, n), carry)[1], 0)

    def scatter_far(items):
        lax.fori_loop(0, 8, lambda n, carry: (send_far(items, n), carry)[1], 0)
        keep_own(items)

    def scatter(items):
        def one(n, carry):
            send_far(items, n)
            send_near(items, n)
            return carry

        send_far(items, 0)
        lax.fori_loop(1, 8, one, 0)
        keep_own(items)

    def gathered(items):
        def one(k, carry):
            peer = plus(s, k, 16)
            for msg, src, dst, cols in items:
                from_peer(msg, src, dst, peer, cols).wait_recv()
            return carry

        lax.fori_loop(1, 16, one, 0)

    def drained(items):
        def one(k, carry):
            peer = plus(s, k, 16)
            for msg, src, dst, cols in items:
                to_peer(msg, src, dst, peer, cols).wait_send()
            return carry

        lax.fori_loop(1, 16, one, 0)

    thirds = [pl.ds(384 * c, 384) for c in range(3)]
    qkv_items = [
        [
            (MQ + 3 * c, qt, rq, thirds[c]),
            (MQ + 3 * c + 1, kt, rk, thirds[c]),
            (MQ + 3 * c + 2, vt, rv, thirds[c]),
        ]
        for c in range(3)
    ]
    tq_items = [(MTQ, tq, rtq, None)]
    a_items = [(MA, over, ra, None), (MTA, ta, rta, None)]
    o_items = [[(MO + c, ot, ro, thirds[c])] for c in range(3)]
    to_items = [(MTO, to, rto, None)]
    g_items = [
        [
            (MG + 3 * c, gq, rgq, thirds[c]),
            (MG + 3 * c + 1, gk, rgk, thirds[c]),
            (MG + 3 * c + 2, gv, rgv, thirds[c]),
        ]
        for c in range(3)
    ]
    tg_items = [(MTG, tg, rtg, None)]

    def w_copy(src, slot, k, who):
        return pltpu.make_async_remote_copy(
            src_ref=src, dst_ref=wb.at[core, slot], send_sem=wsend.at[k], recv_sem=wrecv.at[slot],
            device_id=who, device_id_type=MESH,
        )

    def w_start():
        for n, k in enumerate((1, 7, 2 + 4 * core)):
            w_copy(w_own, chip, n, along_z(k)).start()
        for k in range(1, 4):
            w_copy(w_own, chip, 2 + k, device(plus(x, k, 4), zl, core, zh, y)).start()
        wb[core, chip] = w_own[...]

    def w_core(group):
        part = wb.at[core, pl.ds(4 * group, 4)]
        return pltpu.make_async_remote_copy(
            src_ref=part, dst_ref=part, send_sem=csend.at[group], recv_sem=crecv.at[group],
            device_id=sibling, device_id_type=MESH,
        )

    def w_other(group):
        part = wb.at[1 - core, pl.ds(4 * group, 4)]
        return pltpu.make_async_remote_copy(
            src_ref=part, dst_ref=part, send_sem=csend.at[group], recv_sem=crecv.at[group],
            device_id=sibling, device_id_type=MESH,
        )

    def w_forward():
        for j in range(1, 4):
            slot = x * 4 + plus(zl, j, 4)
            part = wb.at[core, slot]
            w_copy(part, slot, 0, sibling).wait_recv()
            for k in range(1, 4):
                who = device(plus(x, k, 4), zl, core, zh, y)
                w_copy(part, slot, 3 * j + 2 + k, who).start()
        w_core(x).start()

    def w_share():
        for k in range(1, 4):
            group = plus(x, k, 4)
            for j in range(4):
                slot = group * 4 + j
                w_copy(wb.at[core, slot], slot, 0, sibling).wait_recv()
            w_core(group).start()

    def w_finish():
        for group in range(4):
            w_other(group).wait_recv()

        def lay(i, carry):
            slots = [wb[0, 2 * i], wb[1, 2 * i], wb[0, 2 * i + 1], wb[1, 2 * i + 1]]
            w[pl.ds(pl.multiple_of(144 * i, 16), 144), :] = jnp.concatenate(slots, axis=0)
            return carry

        lax.fori_loop(0, 8, lay, 0)

    def w_drained():
        for k in range(6):
            w_copy(w_own, chip, k, sibling).wait_send()
        for k in range(6, 15):
            w_copy(w_own, chip, k, sibling).wait_send()
        for group in range(4):
            w_core(group).wait_send()

    def packer():
        i, m = iota((128, 96), 0), iota((128, 96), 1)
        r = lax.rem(i, 8)
        source = 32 * (r // 2) + 2 * (i // 8) + lax.rem(r, 2)
        return jnp.where(jnp.logical_and(m == source, r < 6), 1.0, 0.0).astype(BF)

    def unpacker(k):
        i, m = iota((32, 128), 0), iota((32, 128), 1)
        return jnp.where(m == 8 * (i // 2) + 2 * k + lax.rem(i, 2), 1.0, 0.0).astype(BF)

    every = pl.ds(0, D)

    def last_rows(part, cols):
        value = part[16:20, :, cols]
        return value.reshape(32, value.shape[2])

    def whole(ref):
        return ref[...].reshape(128, ref.shape[2])

    def pack(stack, dst):
        dst[...] = dot_nn(packer(), stack).astype(BF).reshape(dst.shape)

    def unpack(src, k, part, cols):
        part[16:20, :, cols] = dot_nn(unpacker(k), whole(src)).astype(BF).reshape(4, 8, src.shape[2])

    def pack_arrays(parts, dst):
        pack(jnp.concatenate([last_rows(p, every) for p in parts], axis=0), dst)

    def unpack_arrays(src, parts):
        for k, part in enumerate(parts):
            unpack(src, k, part, every)

    def pack_thirds(part, dst):
        pack(jnp.concatenate([last_rows(part, thirds[g]) for g in range(3)], axis=0), dst)

    def unpack_thirds(src, part):
        for g in range(3):
            unpack(src, g, part, thirds[g])

    def in_thirds(step):
        def one(c, carry):
            step(pl.ds(pl.multiple_of(384 * c, 128), 384))
            return carry

        lax.fori_loop(0, 3, one, 0)

    i, m = iota((TOK, TOK), 0), iota((TOK, TOK), 1)
    patch_i = jnp.where(i < MAIN, lax.rem(i, 8), 8 + lax.rem(i, 2))
    patch_m = jnp.where(m < MAIN, lax.rem(m, 8), 8 + lax.rem(m, 2))
    bias[...] = jnp.where(patch_i == patch_m, 0.0, -1e30)
    for load in loads[:4]:
        load.wait()
    pack_arrays([qt, kt, vt], tq)
    pl.semaphore_wait(barrier, 28)
    w_start()
    scatter_near(tq_items)
    for c in range(3):
        scatter_near(qkv_items[c])
    for load in loads[4:]:
        load.wait()

    def space_forward(h):
        forward_head(h, qs, ks, vs, None, probs_s, space)

    for_heads(0, 8, space_forward)
    w_forward()
    scatter_far(tq_items)
    for c in range(3):
        scatter_far(qkv_items[c])
    for_heads(8, 16, space_forward)
    w_share()
    w_finish()

    def project_space(cols):
        product = dot_nn(get(space, every), w[:, cols])
        put(gradp, cols, product - get(target, cols).astype(F32))

    in_thirds(project_space)

    def back_space(cols):
        put(over, cols, dot_nt(get(gradp, every), w[cols, :]))

    in_thirds(back_space)
    pack_thirds(over, ta)
    scatter_near(a_items)

    gathered(tq_items)
    unpack_arrays(rtq, [rq, rk, rv])

    def time_forward(last):
        return lambda h: forward_head(h, rq, rk, rv, bias, probs_t, ot, last)

    gathered(qkv_items[0])
    for_heads(0, 5, time_forward(1))
    gathered(qkv_items[1])
    scatter_far(a_items)
    for_heads(5, 10, time_forward(4))
    scatter(o_items[0])
    gathered(qkv_items[2])
    for_heads(10, 12, time_forward(7))
    scatter(o_items[1])
    for_heads(12, 16, time_forward(7))
    pack_thirds(ot, to)
    scatter(o_items[2] + to_items)

    def project_time(cols):
        put(gradt, cols, dot_nn(get(ot, every), w[:, cols]))

    in_thirds(project_time)

    def back_time(cols):
        share = dot_nt(get(gradt, every), w[cols, :])
        put(step_b, cols, share + get(ra, cols).astype(F32))

    def time_backward(h):
        backward_head(h, rq, rk, rv, probs_t, step_b, gq, gk, gv)

    def send_grads(c):
        scatter(g_items[c])

    gathered(a_items)
    unpack_thirds(rta, ra)
    in_thirds(back_time)
    for_heads(0, 6, time_backward)
    send_grads(0)

    gathered(to_items)
    for c in range(3):
        gathered(o_items[c])
    unpack_thirds(rto, ro)
    comb[...] = (space[...].astype(F32) + ro[...].astype(F32)).astype(BF)

    def project_all(cols):
        product = dot_nn(get(comb, every), w[:, cols])
        put(gradp, cols, product - get(target, cols).astype(F32))

    in_thirds(project_all)

    def to_sibling(j):
        rows = pl.ds(pl.multiple_of(576 * (1 - core) + 144 * j, 16), 144)
        return pltpu.make_async_remote_copy(
            src_ref=wgp.at[rows], dst_ref=r1.at[pl.ds(144 * j, 144)],
            send_sem=rsend.at[j], recv_sem=rrecv.at[j], device_id=sibling, device_id_type=MESH,
        )

    def x_window(x_):
        return pl.ds(pl.multiple_of(256 * x_, 128), 256)

    ninth = pl.ds(1024, 128)

    def to_x(j, k):
        x_ = plus(x, k, 4)
        rows = pl.ds(144 * j, 144)
        return pltpu.make_async_remote_copy(
            src_ref=half.at[rows, x_window(x_)], dst_ref=r2.at[k - 1, rows],
            send_sem=rsend.at[4 + 3 * j + k - 1], recv_sem=rrecv.at[4 + 3 * j + k - 1],
            device_id=device(x_, zl, core, zh, y), device_id_type=MESH,
        )

    def to_x_ninth(k):
        x_ = plus(x, k, 4)
        return pltpu.make_async_remote_copy(
            src_ref=half.at[pl.ds(pl.multiple_of(144 * x_, 16), 144), ninth], dst_ref=r2n.at[k - 1],
            send_sem=rsend.at[39 + k], recv_sem=rrecv.at[39 + k],
            device_id=device(x_, zl, core, zh, y), device_id_type=MESH,
        )

    def to_y(k):
        y_ = plus(y, k, 8)
        return pltpu.make_async_remote_copy(
            src_ref=h2.at[y_], dst_ref=r3.at[k - 1],
            send_sem=rsend.at[15 + k], recv_sem=rrecv.at[15 + k],
            device_id=device(x, zl, core, zh, y_), device_id_type=MESH,
        )

    def to_y_ninth(n):
        y_ = 2 * x + n
        slot = plus(y, 15 - y_, 8)
        return pltpu.make_async_remote_copy(
            src_ref=n2.at[n], dst_ref=r3n.at[slot], send_sem=rsend.at[43 + n],
            recv_sem=rrecv.at[45 + slot], device_id=device(x, zl, core, zh, y_), device_id_type=MESH,
        )

    def from_y_ninth(slot):
        return pltpu.make_async_remote_copy(
            src_ref=n2.at[0], dst_ref=r3n.at[slot], send_sem=rsend.at[43],
            recv_sem=rrecv.at[45 + slot], device_id=sibling, device_id_type=MESH,
        )

    def to_z(k, same, ninth_=False):
        zh_ = zh if same else 1 - zh
        slot = k - 1 if same else 3 + k
        src, dst, sem = (h3n, r4n, 52) if ninth_ else (h3, r4, 23)
        return pltpu.make_async_remote_copy(
            src_ref=src, dst_ref=dst.at[slot], send_sem=rsend.at[sem + slot],
            recv_sem=rrecv.at[sem + slot], device_id=device(x, plus(zl, k, 4), core, zh_, y),
            device_id_type=MESH,
        )

    def final_peer(k, flip):
        return device(plus(x, k, 4), zl, core if flip == 0 else 1 - core, zh, y)

    def to_all(k, flip):
        slot = k - 1 if flip == 0 else 3 + k
        return pltpu.make_async_remote_copy(
            src_ref=h4, dst_ref=r5.at[x], send_sem=rsend.at[31 + slot], recv_sem=rrecv.at[31 + x],
            device_id=final_peer(k, flip), device_id_type=MESH,
        )

    def to_all_ninth(k, flip):
        slot = k - 1 if flip == 0 else 3 + k
        return pltpu.make_async_remote_copy(
            src_ref=h4n, dst_ref=r5n, send_sem=rsend.at[59 + slot], recv_sem=rrecv.at[59],
            device_id=final_peer(k, flip), device_id_type=MESH,
        )

    def from_all(x_):
        return pltpu.make_async_remote_copy(
            src_ref=h4, dst_ref=r5.at[x_], send_sem=rsend.at[31], recv_sem=rrecv.at[31 + x_],
            device_id=sibling, device_id_type=MESH,
        )

    everyone = [(k, 0) for k in range(1, 4)] + [(k, 1) for k in range(4)]
    around_z = [(k, True) for k in range(1, 4)] + [(k, False) for k in range(4)]
    here = zh == core
    owner = y // 2 == x

    def terms(i, carry):
        j = core * i + (1 - core) * (8 - i)
        rows = pl.ds(pl.multiple_of(128 * j, 128), 128)
        wgp[rows, :] = dot_tn(get(comb, rows), get(gradp, every)).astype(BF)
        return carry

    def back_all(cols):
        put(step_f, cols, dot_nt(get(gradp, every), w[cols, :]))

    lax.fori_loop(0, 5, terms, 0)
    for j in range(4):
        to_sibling(j).start()
    lax.fori_loop(5, 9, terms, 0)

    for_heads(6, 12, time_backward)
    send_grads(1)

    for j in range(4):
        to_sibling(j).wait_recv()
        rows = pl.ds(144 * j, 144)
        own = wgp[pl.ds(pl.multiple_of(576 * core + 144 * j, 16), 144), :]
        half[rows, :] = (own.astype(F32) + r1[rows, :].astype(F32)).astype(BF)
        for k in range(1, 4):
            to_x(j, k).start()

    for k in range(1, 4):
        to_x_ninth(k).start()
    for_heads(12, 16, time_backward)
    send_grads(2)
    pack_arrays([gq, gk, gv], tg)
    scatter(tg_items)

    def space_backward(h):
        backward_head(h, qs, ks, vs, probs_s, step_f, gqs, gks, gvs)

    in_thirds(back_all)
    for_heads(0, 16, space_backward)

    for j in range(4):
        for k in range(1, 4):
            to_x(j, k).wait_recv()
        for i in range(2):
            rows = pl.ds(144 * j + 72 * i, 72)
            total = half[rows, x_window(x)].astype(F32)
            for k in range(1, 4):
                total = total + r2[k - 1, rows, :].astype(F32)
            h2[2 * j + i] = total.astype(BF)
    for k in (1, 7, 2, 6, 3, 5, 4):
        to_y(k).start()
    total = half[pl.ds(pl.multiple_of(144 * x, 16), 144), ninth].astype(F32)
    for k in range(1, 4):
        to_x_ninth(k).wait_recv()
        total = total + r2n[k - 1].astype(F32)
    n2[...] = total.astype(BF).reshape(2, 72, 128)
    for n in range(2):

        @pl.when(y != 2 * x + n)
        def _(n=n):
            to_y_ninth(n).start()

    drained(qkv_items[0] + qkv_items[1] + qkv_items[2])
    drained(tq_items + a_items + to_items + o_items[0] + o_items[1] + o_items[2])
    drained(g_items[0] + g_items[1])
    w_drained()

    total = h2[y].astype(F32)
    for k in range(1, 8):
        to_y(k).wait_recv()
        total = total + r3[k - 1].astype(F32)
    h3[...] = total.astype(BF)

    @pl.when(here)
    def _():
        for k in range(1, 4):
            to_z(k, True).start()

    @pl.when(jnp.logical_not(here))
    def _():
        for k in range(4):
            to_z(k, False).start()

    @pl.when(owner)
    def _():
        total = n2[lax.rem(y, 2)].astype(F32)
        for slot in range(7):
            from_y_ninth(slot).wait_recv()
            total = total + r3n[slot].astype(F32)
        h3n[...] = total.astype(BF)

        @pl.when(here)
        def _():
            for k in range(1, 4):
                to_z(k, True, True).start()

        @pl.when(jnp.logical_not(here))
        def _():
            for k in range(4):
                to_z(k, False, True).start()

    @pl.when(here)
    def _():
        total = h3[...].astype(F32)
        for n, (k, same) in enumerate(around_z):
            to_z(k, same).wait_recv()
            total = total + r4[n].astype(F32)
        h4[...] = total.astype(BF)
        for k, flip in everyone:
            to_all(k, flip).start()
        r5[x] = h4[...]

        @pl.when(owner)
        def _():
            total = h3n[...].astype(F32)
            for n, (k, same) in enumerate(around_z):
                to_z(k, same, True).wait_recv()
                total = total + r4n[n].astype(F32)
            h4n[...] = total.astype(BF)
            for k, flip in everyone:
                to_all_ninth(k, flip).start()
            r5n[...] = h4n[...]

        @pl.when(jnp.logical_not(owner))
        def _():
            to_all_ninth(0, 1).wait_recv()

        for k in range(1, 4):
            from_all(plus(x, k, 4)).wait_recv()
        for k in range(1, 4):
            to_z(k, True).wait_send()
        for k, flip in everyone:
            to_all(k, flip).wait_send()

        @pl.when(owner)
        def _():
            for k in range(1, 4):
                to_z(k, True, True).wait_send()
            for k, flip in everyone:
                to_all_ninth(k, flip).wait_send()

    @pl.when(jnp.logical_not(here))
    def _():
        for k in range(4):
            from_all(plus(x, k, 4)).wait_recv()
        to_all_ninth(0, 1).wait_recv()
        for k in range(4):
            to_z(k, False).wait_send()

        @pl.when(owner)
        def _():
            for k in range(4):
                to_z(k, False, True).wait_send()

    for c in range(4):
        sums[:, pl.ds(256 * c, 256)] = r5[c]
    sums[:, ninth] = r5n[...]

    for c in range(3):
        gathered(g_items[c])
    gathered(tg_items)
    for src, dst in ((rgq, rgq_out), (rgk, rgk_out), (rgv, rgv_out), (rtg, rtg_out)):
        dst[...] = src[...]

    drained(g_items[2] + tg_items)
    for j in range(4):
        to_sibling(j).wait_send()
        for k in range(1, 4):
            to_x(j, k).wait_send()
    for k in range(1, 4):
        to_x_ninth(k).wait_send()
    for k in range(1, 8):
        to_y(k).wait_send()
    for n in range(2):

        @pl.when(y != 2 * x + n)
        def _(n=n):
            to_y_ninth(n).wait_send()


def finish(gqs, gks, gvs, rgq, rgk, rgv, rtg, sums, *out):
    for src, dst in zip((gqs, gks, gvs), out[:3]):
        dst[...] = src[...]
    packed = rtg[...].reshape(128, D)
    for k, (src, dst) in enumerate(zip((rgq, rgk, rgv), out[3:6])):
        i, m = iota((32, 128), 0), iota((32, 128), 1)
        chosen = jnp.where(m == 8 * (i // 2) + 2 * k + lax.rem(i, 2), 1.0, 0.0).astype(BF)
        dst[0:16] = src[...]
        dst[16:20] = dot_nn(chosen, packed).astype(BF).reshape(4, 8, D)
    out[6][...] = sums[...].astype(F32) * (1.0 / math.sqrt(81920))


def shards(q_space, k_space, v_space, q_time, k_time, v_time, weight, target):
    tokens = (q_space, k_space, v_space, q_time, k_time, v_time, target)
    flat = [item.reshape(20, 8, D) for item in tokens]
    vm = pl.BlockSpec(memory_space=pltpu.VMEM)
    anywhere = pl.BlockSpec(memory_space=pltpu.HBM)

    def buf(*shape, dtype=BF):
        return pltpu.VMEM(shape, dtype)

    tok = buf(20, 8, D)
    main = buf(16, 8, D)
    third = buf(16, 8, 384)
    scratch = [
        tok, tok, tok, tok, tok, tok, buf(36, D), tok,
        buf(2, 16, 36, D), buf(D, D),
        tok, tok, tok, tok,
        main, third, main, third, third, main,
        tok, tok, tok, tok,
        tok, tok, third, tok, tok, tok,
        tok, tok, tok, main, main, main, main,
        buf(HEADS, TOK, TOK, dtype=F32), buf(HEADS, TOK, TOK, dtype=F32), buf(TOK, TOK, dtype=F32),
        buf(D, D), buf(576, D), buf(576, D), buf(3, 576, 256), buf(3, 144, 128),
        buf(8, 72, 256), buf(2, 72, 128), buf(7, 72, 256), buf(7, 72, 128),
        buf(72, 256), buf(72, 128), buf(7, 72, 256), buf(7, 72, 128),
        buf(72, 256), buf(72, 128), buf(4, 72, 256), buf(72, 128),
        pltpu.SemaphoreType.DMA((8,)),
        pltpu.SemaphoreType.DMA((N_MSG, 16)), pltpu.SemaphoreType.DMA((N_MSG, 16)),
        pltpu.SemaphoreType.DMA((15,)), pltpu.SemaphoreType.DMA((16,)),
        pltpu.SemaphoreType.DMA((4,)), pltpu.SemaphoreType.DMA((4,)),
        pltpu.SemaphoreType.DMA((68,)), pltpu.SemaphoreType.DMA((68,)),
    ]
    out = jax.ShapeDtypeStruct((20, 8, D), BF)
    part = jax.ShapeDtypeStruct((16, 8, D), BF)
    middle = pl.pallas_call(
        kernel,
        out_shape=[out] * 3 + [part] * 4 + [jax.ShapeDtypeStruct((72, D), BF)],
        in_specs=[anywhere] * 8,
        out_specs=[vm] * 8,
        scratch_shapes=scratch,
        compiler_params=pltpu.CompilerParams(
            collective_id=0, has_side_effects=True, vmem_limit_bytes=56 * 1024 * 1024
        ),
        name="step",
    )(*flat[:6], weight, flat[6])
    results = pl.pallas_call(
        finish,
        out_shape=[out] * 6 + [jax.ShapeDtypeStruct((72, D), F32)],
        in_specs=[vm] * 8,
        out_specs=[vm] * 7,
        compiler_params=pltpu.CompilerParams(vmem_limit_bytes=60 * 1024 * 1024),
        name="finish",
    )(*middle)
    return tuple(item.reshape(q_space.shape) for item in results[:6]) + (results[6],)


def solution(mesh):
    token = P("dp", "seq", None)
    return jax.shard_map(
        shards,
        mesh=mesh,
        in_specs=(token,) * 6 + (P("dp", None), token),
        out_specs=(token,) * 6 + (P("seq", None),),
        check_vma=False,
    )
```
